128 devices in a mesh: tm: 4 (over z_hi, core), chan: 32 (over x, y, z_lo).
Axes of the slice: x: 4, y: 4, z: 4 (z_hi: 2, z_lo: 2; z = z_hi * 2 + z_lo), core: 2. Of those that a mesh axis runs over, the one named last changes fastest.
Arguments:
- voltages: float32 [512, 262144], P('chan', 'tm'), may hold values from -6 to 6
- fir_taps: float32 [4, 2048], replicated, may hold values from -3 to 3
Outputs:
- visibilities: float32 [1024, 2, 512, 512], P(('tm', 'chan'))
The draws below stay inside these ranges and needn't reach their ends.
All inputs are finite; a program needn't handle non-finite values.
Results may differ from the reference program's by a relative error of at most 0.00009.
Values sent between devices are 32-bit elements; how exact they have to be, the bound alone decides.
A program may use at most 128 MiB of HBM per device.

```python
import jax
import jax.numpy as jnp
from jax import lax

INPUTS = 512
CHANNELS = 1024
TAPS = 4
FRAME = 2048
SPECTRA = 128
SAMPLES = 262144


def block_levels(stream_key, shape, pieces, least, largest):
    gain = 1.0
    for position, parts in pieces:
        draws = jax.random.uniform(jax.random.fold_in(jax.random.fold_in(stream_key, 6), position), (parts,), jnp.float32, least / len(pieces), largest / len(pieces))
        gain = gain * jnp.repeat(jnp.exp(draws), shape[position] // parts).reshape((-1,) + (1,) * (len(shape) - 1 - position))
    return gain


def scatter_about(own_key, extent, width, reach, split=(), held_as=jnp.bfloat16):
    gain = block_levels(own_key, extent, split, -0.22, 0.18) if split else 1.0
    drawn = jax.random.normal(own_key, extent, jnp.float32) * width * gain
    return jnp.minimum(jnp.maximum(drawn, -reach), reach).astype(held_as)


def setup_inputs(seed: int = 0) -> dict:
    splits = jax.random.split(jax.random.key(seed), 3)
    voltages = scatter_about(splits[0], (INPUTS, SAMPLES), 1.0, 6.0, ((0, 32), (1, 4)), jnp.float32)
    fir_taps = scatter_about(splits[1], (TAPS, FRAME), TAPS ** -0.5, 3.0, (), jnp.float32)
    return {"voltages": voltages, "fir_taps": fir_taps}


def correlate_one(owned):
    stacked = jnp.concatenate([owned[0], owned[1]], axis=1)
    turned = jnp.concatenate([owned[1], -owned[0]], axis=1)
    both = jnp.concatenate([stacked, turned], axis=0)
    gram = jnp.dot(both, stacked.T, precision=lax.Precision.HIGHEST) * (1.0 / SPECTRA)
    return gram.reshape(2, INPUTS, INPUTS)

def reference(voltages, fir_taps):
    frames = voltages.reshape(INPUTS, SPECTRA, FRAME)
    padded = jnp.concatenate([jnp.zeros((INPUTS, TAPS - 1, FRAME), jnp.float32), frames], axis=1)
    filtered = jnp.zeros((INPUTS, SPECTRA, FRAME), jnp.float32)
    for tap in range(TAPS):
        start = TAPS - 1 - tap
        filtered = filtered + fir_taps[tap] * padded[:, start:start + SPECTRA, :]
    spectrum = jnp.fft.rfft(filtered, axis=2)[:, :, :CHANNELS]
    scale = 1.0 / jnp.sqrt(jnp.float32(FRAME))
    real_part = (jnp.real(spectrum) * scale).astype(jnp.float32)
    imag_part = (jnp.imag(spectrum) * scale).astype(jnp.float32)
    stacked = jnp.stack([real_part, imag_part], axis=0)
    per_channel = jnp.transpose(stacked, (3, 0, 1, 2))
    return lax.map(correlate_one, per_channel)
```

```python
import functools

import jax
import jax.numpy as jnp
import numpy as np
from jax import lax
from jax.experimental import pallas as pl
from jax.experimental.pallas import tpu as pltpu
from jax.sharding import PartitionSpec as P

MESH = pl.DeviceIdType.MESH
DEVICES = 128
GROUP = 16
LANES = 128


def tables(frame, scale):
    half = frame // 2
    sample = np.arange(half)

    def angle(k):
        return 2.0 * np.pi * ((k[:, None] * sample) % frame) / frame

    base = []
    for parity in range(2):
        wave = angle(2 * np.arange(4) + parity)
        cos, sin = np.cos(wave) * scale, np.sin(wave) * scale
        base.append(np.stack([cos, -sin], axis=1).reshape(8, half))
        base.append(np.stack([-sin, -cos], axis=1).reshape(8, half))
    turn = angle(8 * np.arange(DEVICES))
    rot = np.stack([np.cos(turn), np.sin(turn)])
    return np.stack(base).astype(np.float32), rot.astype(np.float32)


def coordinates():
    tm = lax.axis_index("tm")
    chan = lax.axis_index("chan")
    return chan // 8, (chan // 2) % 4, (tm // 2) * 2 + chan % 2, tm % 2


def target(t, place):
    x, y, z, core = place
    x = (x + t) % 4
    y = (y + t // 4 + t) % 4
    z = (z + t // 16 + t // 4 + t) % 4
    core = (core + t // 64 + t) % 2
    return (z // 2) * 2 + core, (x * 4 + y) * 2 + z % 2


def split(value):
    high = value.astype(jnp.bfloat16)
    return high, (value - high.astype(jnp.float32)).astype(jnp.bfloat16)


def turned_dot(a, b):
    return lax.dot_general(a, b, (((1,), (1,)), ((), ())), preferred_element_type=jnp.float32)


def spectra_kernel(
    volt, halo, taps, base, rot, out, vbuf, even, odd, fh, fl, th, tl, buf, in_sem, send_sem, recv_sem, own_sem
):
    inputs = volt.shape[0]
    frame = taps.shape[1]
    half = frame // 2
    edge = halo.shape[1]
    spec = volt.shape[1] // frame
    place = coordinates()
    me = lax.axis_index("tm") * 32 + lax.axis_index("chan")

    pieces = 4
    width = volt.shape[1] // pieces
    loads = [pltpu.make_async_copy(halo, vbuf.at[:, pl.ds(0, edge)], in_sem.at[pieces])]
    for piece in range(pieces):
        loads.append(
            pltpu.make_async_copy(
                volt.at[:, pl.ds(piece * width, width)],
                vbuf.at[:, pl.ds(edge + piece * width, width)],
                in_sem.at[piece],
            )
        )
    for load in loads:
        load.start()

    barrier = pltpu.get_barrier_semaphore()

    def greet(t, carry):
        other = (me + t) % DEVICES
        pl.semaphore_signal(barrier, 1, device_id=(other // 32, other % 32), device_id_type=MESH)
        return carry

    lax.fori_loop(1, DEVICES, greet, 0)
    for load in loads:
        load.wait()

    def filter_block(block, carry):
        low = pl.multiple_of(block * LANES, LANES)
        high = pl.multiple_of(half + block * LANES, LANES)
        weights = [
            (
                jnp.broadcast_to(taps[pl.ds(tap, 1), pl.ds(low, LANES)], (inputs, LANES)),
                jnp.broadcast_to(taps[pl.ds(tap, 1), pl.ds(high, LANES)], (inputs, LANES)),
            )
            for tap in range(4)
        ]
        past = []
        for step in range(spec + 3):
            now = (
                vbuf[:, pl.ds(pl.multiple_of(step * frame + low, LANES), LANES)],
                vbuf[:, pl.ds(pl.multiple_of(step * frame + high, LANES), LANES)],
            )
            past = [now] + past[:3]
            if step < 3:
                continue
            a = past[0][0] * weights[0][0]
            b = past[0][1] * weights[0][1]
            for tap in range(1, 4):
                a = a + past[tap][0] * weights[tap][0]
                b = b + past[tap][1] * weights[tap][1]
            even[pl.ds(step - 3, inputs, stride=spec), :] = a + b
            odd[pl.ds(step - 3, inputs, stride=spec), :] = a - b
        for parity, source in enumerate((even, odd)):
            for start in range(0, inputs * spec, LANES):
                rows = pl.ds(start, LANES)
                upper, lower = split(source[rows, :])
                fh[parity, rows, pl.ds(low, LANES)] = upper
                fl[parity, rows, pl.ds(low, LANES)] = lower
        return carry

    lax.fori_loop(0, half // LANES, filter_block, 0)

    pl.semaphore_wait(barrier, DEVICES - 1)

    def chunk(c, carry):
        def table_rows(pair, inner):
            rows = pl.ds(pl.multiple_of(pair * 16, 16), 16)
            turns = []
            for k in range(2):
                tm, chan = target(c * GROUP + pair * 2 + k, place)
                device = tm * 32 + chan
                turns.append((rot[0, pl.ds(device, 1), :], rot[1, pl.ds(device, 1), :]))
            for parity in range(2):
                value = jnp.concatenate(
                    [base[2 * parity] * cos + base[2 * parity + 1] * sin for cos, sin in turns], axis=0
                )
                high, low = split(value)
                th[parity, rows, :] = high
                tl[parity, rows, :] = low
            return inner

        lax.fori_loop(0, GROUP // 2, table_rows, 0)
        slots = pl.ds(c * GROUP, GROUP)
        for parity in range(2):
            high = fh[parity]
            value = turned_dot(th[parity], high) + turned_dot(tl[parity], high) + turned_dot(th[parity], fl[parity])
            buf[slots, parity] = value.reshape(GROUP, 8, inputs * spec)

        def send(k, inner):
            t = c * GROUP + k

            @pl.when(t > 0)
            def _():
                pltpu.make_async_remote_copy(
                    src_ref=buf.at[t],
                    dst_ref=out.at[me],
                    send_sem=send_sem,
                    recv_sem=recv_sem,
                    device_id=target(t, place),
                    device_id_type=MESH,
                ).start()

            return inner

        lax.fori_loop(0, GROUP, send, 0)
        return carry

    lax.fori_loop(0, DEVICES // GROUP, chunk, 0)
    own = pltpu.make_async_copy(buf.at[0], out.at[me], own_sem)
    own.start()
    own.wait()
    rest = pl.ds(0, DEVICES - 1)
    pltpu.make_async_remote_copy(
        src_ref=buf.at[rest],
        dst_ref=out.at[rest],
        send_sem=send_sem,
        recv_sem=recv_sem,
        device_id=target(1, place),
        device_id_type=MESH,
    ).wait()


def regroup(blocks, lane):
    first = lane < 64
    stage = [
        jnp.where(first, blocks[0], pltpu.roll(blocks[2], 64, 1)),
        jnp.where(first, blocks[1], pltpu.roll(blocks[3], 64, 1)),
        jnp.where(first, pltpu.roll(blocks[0], 64, 1), blocks[2]),
        jnp.where(first, pltpu.roll(blocks[1], 64, 1), blocks[3]),
    ]
    even = (lane // 32) % 2 == 0
    result = []
    for left, right in ((stage[0], stage[1]), (stage[2], stage[3])):
        result.append(jnp.where(even, left, pltpu.roll(right, 32, 1)))
        result.append(jnp.where(even, pltpu.roll(left, 96, 1), right))
    return result


def gram_kernel(owned, out, held):
    @pl.when(pl.program_id(1) == 0)
    def _():
        lane = lax.broadcasted_iota(jnp.int32, (8, LANES), 1)

        def sender(n, carry):
            for g in range(4):
                lanes = pl.ds(g * LANES, LANES)
                parts = regroup([owned[tm * 32 + n, 0, :, lanes] for tm in range(4)], lane)
                for a in range(4):
                    held[pl.ds(n * 16 + g * 4 + a, 8, stride=512), :] = parts[a]
            return carry

        lax.fori_loop(0, 32, sender, 0)

    q = pl.program_id(1)
    re = held[pl.ds(pl.multiple_of(q * 1024, 512), 512), :]
    im = held[pl.ds(pl.multiple_of(q * 1024 + 512, 512), 512), :]
    (re_h, re_l), (im_h, im_l) = split(re), split(im)
    right_h = jnp.concatenate([re_h, im_h], axis=1)
    right_l = jnp.concatenate([re_l, im_l], axis=1)
    turned_h = jnp.concatenate([im_h, -re_h], axis=1)
    turned_l = jnp.concatenate([im_l, -re_l], axis=1)
    for part, (high, low) in enumerate(((right_h, right_l), (turned_h, turned_l))):
        out[0, part] = turned_dot(high, right_h) + turned_dot(low, right_h) + turned_dot(high, right_l)


def body(voltages, fir_taps):
    inputs = voltages.shape[0]
    frame = fir_taps.shape[1]
    half = frame // 2
    edge = (fir_taps.shape[0] - 1) * frame
    spec = voltages.shape[1] // frame
    rows = inputs * spec
    count = lax.axis_size("tm")
    halo = lax.ppermute(voltages[:, voltages.shape[1] - edge :], "tm", [(i, i + 1) for i in range(count - 1)])
    base, rot = tables(frame, 1.0 / 512.0)
    vmem = pl.BlockSpec(memory_space=pltpu.VMEM)
    anywhere = pl.BlockSpec(memory_space=pl.ANY)
    owned = pl.pallas_call(
        spectra_kernel,
        out_shape=jax.ShapeDtypeStruct((DEVICES, 2, 8, rows), jnp.float32),
        in_specs=[anywhere, anywhere, vmem, vmem, vmem],
        out_specs=anywhere,
        scratch_shapes=[
            pltpu.VMEM((inputs, edge + voltages.shape[1]), jnp.float32),
            pltpu.VMEM((rows, LANES), jnp.float32),
            pltpu.VMEM((rows, LANES), jnp.float32),
            pltpu.VMEM((2, rows, half), jnp.bfloat16),
            pltpu.VMEM((2, rows, half), jnp.bfloat16),
            pltpu.VMEM((2, GROUP * 8, half), jnp.bfloat16),
            pltpu.VMEM((2, GROUP * 8, half), jnp.bfloat16),
            pltpu.VMEM((DEVICES, 2, 8, rows), jnp.float32),
            pltpu.SemaphoreType.DMA((5,)),
            pltpu.SemaphoreType.DMA,
            pltpu.SemaphoreType.DMA,
            pltpu.SemaphoreType.DMA,
        ],
        compiler_params=pltpu.CompilerParams(
            collective_id=0, has_side_effects=True, vmem_limit_bytes=48 * 1024 * 1024
        ),
        name="spectra",
    )(voltages, halo, fir_taps, base, rot)
    return pl.pallas_call(
        gram_kernel,
        grid=(2, 4),
        out_shape=jax.ShapeDtypeStruct((8, 2, 512, 512), jnp.float32),
        in_specs=[pl.BlockSpec((DEVICES, 1, 8, rows), lambda p, q: (0, p, 0, 0))],
        out_specs=pl.BlockSpec((1, 2, 512, 512), lambda p, q: (2 * q + p, 0, 0, 0)),
        scratch_shapes=[pltpu.VMEM((8 * 512, LANES), jnp.float32)],
        compiler_params=pltpu.CompilerParams(
            dimension_semantics=("arbitrary", "arbitrary"), vmem_limit_bytes=48 * 1024 * 1024
        ),
        name="gram",
    )(owned)


def solution(mesh):
    return jax.shard_map(
        body,
        mesh=mesh,
        in_specs=(P("chan", "tm"), P()),
        out_specs=P(("tm", "chan"), None, None, None),
        check_vma=False,
    )
```

```python
import functools

import jax
import jax.numpy as jnp
import numpy as np
from jax import lax
from jax.experimental import pallas as pl
from jax.experimental.pallas import tpu as pltpu
from jax.sharding import PartitionSpec as P

MESH = pl.DeviceIdType.MESH
DEVICES = 128
GROUP = 16
LANES = 128


def tables(frame, scale):
    half = frame // 2
    sample = np.arange(half)

    def angle(k):
        return 2.0 * np.pi * ((k[:, None] * sample) % frame) / frame

    base = []
    for parity in range(2):
        wave = angle(2 * np.arange(4) + parity)
        cos, sin = np.cos(wave) * scale, np.sin(wave) * scale
        base.append(np.stack([cos, -sin], axis=1).reshape(8, half))
        base.append(np.stack([-sin, -cos], axis=1).reshape(8, half))
    turn = angle(8 * np.arange(DEVICES))
    rot = np.stack([np.cos(turn), np.sin(turn)])
    return np.stack(base).astype(np.float32), rot.astype(np.float32)


def coordinates():
    tm = lax.axis_index("tm")
    chan = lax.axis_index("chan")
    return chan // 8, (chan // 2) % 4, (tm // 2) * 2 + chan % 2, tm % 2


def target(t, place):
    x, y, z, core = place
    x = (x + t) % 4
    y = (y + t // 4 + t) % 4
    z = (z + t // 16 + t // 4 + t) % 4
    core = (core + t // 64 + t) % 2
    return (z // 2) * 2 + core, (x * 4 + y) * 2 + z % 2


def split(value):
    high = value.astype(jnp.bfloat16)
    return high, (value - high.astype(jnp.float32)).astype(jnp.bfloat16)


def turned_dot(a, b):
    return lax.dot_general(a, b, (((1,), (1,)), ((), ())), preferred_element_type=jnp.float32)


def spectra_kernel(
    volt, halo, taps_in, base_in, rot_in, out, taps, base, rot, vbuf, even, odd, fh, fl, th, tl, buf, in_sem, send_sem, recv_sem, own_sem
):
    inputs = volt.shape[0]
    frame = taps_in.shape[1]
    half = frame // 2
    edge = halo.shape[1]
    spec = volt.shape[1] // frame
    place = coordinates()
    me = lax.axis_index("tm") * 32 + lax.axis_index("chan")

    pieces = 4
    width = volt.shape[1] // pieces
    loads = [pltpu.make_async_copy(halo, vbuf.at[:, pl.ds(0, edge)], in_sem.at[pieces])]
    for piece in range(pieces):
        loads.append(
            pltpu.make_async_copy(
                volt.at[:, pl.ds(piece * width, width)],
                vbuf.at[:, pl.ds(edge + piece * width, width)],
                in_sem.at[piece],
            )
        )
    loads.append(pltpu.make_async_copy(taps_in, taps, in_sem.at[pieces + 1]))
    later = [
        pltpu.make_async_copy(base_in, base, in_sem.at[pieces + 2]),
        pltpu.make_async_copy(rot_in, rot, in_sem.at[pieces + 3]),
    ]
    for load in loads + later:
        load.start()

    barrier = pltpu.get_barrier_semaphore()

    def greet(t, carry):
        other = (me + t) % DEVICES
        pl.semaphore_signal(barrier, 1, device_id=(other // 32, other % 32), device_id_type=MESH)
        return carry

    lax.fori_loop(1, DEVICES, greet, 0)
    for load in loads:
        load.wait()

    def filter_block(block, carry):
        low = pl.multiple_of(block * LANES, LANES)
        high = pl.multiple_of(half + block * LANES, LANES)
        weights = [
            (
                jnp.broadcast_to(taps[pl.ds(tap, 1), pl.ds(low, LANES)], (inputs, LANES)),
                jnp.broadcast_to(taps[pl.ds(tap, 1), pl.ds(high, LANES)], (inputs, LANES)),
            )
            for tap in range(4)
        ]
        past = []
        for step in range(spec + 3):
            now = (
                vbuf[:, pl.ds(pl.multiple_of(step * frame + low, LANES), LANES)],
                vbuf[:, pl.ds(pl.multiple_of(step * frame + high, LANES), LANES)],
            )
            past = [now] + past[:3]
            if step < 3:
                continue
            a = past[0][0] * weights[0][0]
            b = past[0][1] * weights[0][1]
            for tap in range(1, 4):
                a = a + past[tap][0] * weights[tap][0]
                b = b + past[tap][1] * weights[tap][1]
            even[pl.ds(step - 3, inputs, stride=spec), :] = a + b
            odd[pl.ds(step - 3, inputs, stride=spec), :] = a - b
        for parity, source in enumerate((even, odd)):
            for start in range(0, inputs * spec, LANES):
                rows = pl.ds(start, LANES)
                upper, lower = split(source[rows, :])
                fh[parity, rows, pl.ds(low, LANES)] = upper
                fl[parity, rows, pl.ds(low, LANES)] = lower
        return carry

    lax.fori_loop(0, half // LANES, filter_block, 0)

    for load in later:
        load.wait()
    pl.semaphore_wait(barrier, DEVICES - 1)

    def chunk(c, carry):
        def table_rows(pair, inner):
            rows = pl.ds(pl.multiple_of(pair * 16, 16), 16)
            turns = []
            for k in range(2):
                tm, chan = target(c * GROUP + pair * 2 + k, place)
                device = tm * 32 + chan
                turns.append((rot[0, pl.ds(device, 1), :], rot[1, pl.ds(device, 1), :]))
            for parity in range(2):
                value = jnp.concatenate(
                    [base[2 * parity] * cos + base[2 * parity + 1] * sin for cos, sin in turns], axis=0
                )
                high, low = split(value)
                th[parity, rows, :] = high
                tl[parity, rows, :] = low
            return inner

        lax.fori_loop(0, GROUP // 2, table_rows, 0)
        slots = pl.ds(c * GROUP, GROUP)
        for parity in range(2):
            high = fh[parity]
            value = turned_dot(th[parity], high) + turned_dot(tl[parity], high) + turned_dot(th[parity], fl[parity])
            buf[slots, parity] = value.reshape(GROUP, 8, inputs * spec)

        def send(k, inner):
            t = c * GROUP + k

            @pl.when(t > 0)
            def _():
                pltpu.make_async_remote_copy(
                    src_ref=buf.at[t],
                    dst_ref=out.at[me],
                    send_sem=send_sem,
                    recv_sem=recv_sem,
                    device_id=target(t, place),
                    device_id_type=MESH,
                ).start()

            return inner

        lax.fori_loop(0, GROUP, send, 0)
        return carry

    lax.fori_loop(0, DEVICES // GROUP, chunk, 0)
    own = pltpu.make_async_copy(buf.at[0], out.at[me], own_sem)
    own.start()
    own.wait()
    rest = pl.ds(0, DEVICES - 1)
    pltpu.make_async_remote_copy(
        src_ref=buf.at[rest],
        dst_ref=out.at[rest],
        send_sem=send_sem,
        recv_sem=recv_sem,
        device_id=target(1, place),
        device_id_type=MESH,
    ).wait()


def regroup(blocks, lane):
    quarter = lane // 32

    def pick(choices):
        low = jnp.where(quarter == 0, choices[0], choices[1])
        high = jnp.where(quarter == 2, choices[2], choices[3])
        return jnp.where(quarter < 2, low, high)

    shifted = []
    for shift in range(4):
        mixed = pick([blocks[(a + shift) % 4] for a in range(4)])
        shifted.append(pltpu.roll(mixed, 32 * shift, 1) if shift else mixed)
    return [pick([shifted[(tm - a) % 4] for tm in range(4)]) for a in range(4)]


def gram_kernel(owned, out, held, pairs):
    @pl.when(pl.program_id(1) == 0)
    def _():
        lane = lax.broadcasted_iota(jnp.int32, (8, LANES), 1)

        def sender(n, carry):
            for g in range(4):
                lanes = pl.ds(g * LANES, LANES)
                parts = regroup([owned[tm * 32 + n, 0, :, lanes] for tm in range(4)], lane)
                for a in range(4):
                    held[pl.ds(pl.multiple_of((n * 16 + g * 4 + a) * 8, 8), 8), :] = parts[a]
            return carry

        lax.fori_loop(0, 32, sender, 0, unroll=2)

        def channel(q, carry):
            re_h, re_l = split(held[pl.ds(q * 2, 512, stride=8), :])
            im_h, im_l = split(held[pl.ds(q * 2 + 1, 512, stride=8), :])
            for kind, (left, right) in enumerate(((re_h, im_h), (re_l, im_l), (im_h, -re_h), (im_l, -re_l))):
                pairs[q, kind, :, :LANES] = left
                pairs[q, kind, :, LANES:] = right
            return carry

        lax.fori_loop(0, 4, channel, 0)

    q = pl.program_id(1)
    right_h, right_l, turned_h, turned_l = (pairs[q, kind] for kind in range(4))
    left = jnp.concatenate([right_h, turned_h, right_l, turned_l], axis=0)
    wide = turned_dot(left, right_h)
    fine = turned_dot(left[:1024], right_l)
    for part in range(2):
        here = slice(part * 512, (part + 1) * 512)
        there = slice((part + 2) * 512, (part + 3) * 512)
        out[0, part] = wide[here] + wide[there] + fine[here]


def body(voltages, fir_taps):
    inputs = voltages.shape[0]
    frame = fir_taps.shape[1]
    half = frame // 2
    edge = (fir_taps.shape[0] - 1) * frame
    spec = voltages.shape[1] // frame
    rows = inputs * spec
    count = lax.axis_size("tm")
    halo = lax.ppermute(voltages[:, voltages.shape[1] - edge :], "tm", [(i, i + 1) for i in range(count - 1)])
    base, rot = tables(frame, 1.0 / 512.0)
    anywhere = pl.BlockSpec(memory_space=pl.ANY)
    owned = pl.pallas_call(
        spectra_kernel,
        out_shape=jax.ShapeDtypeStruct((DEVICES, 2, 8, rows), jnp.float32),
        in_specs=[anywhere] * 5,
        out_specs=anywhere,
        scratch_shapes=[
            pltpu.VMEM(fir_taps.shape, jnp.float32),
            pltpu.VMEM(base.shape, jnp.float32),
            pltpu.VMEM(rot.shape, jnp.float32),
            pltpu.VMEM((inputs, edge + voltages.shape[1]), jnp.float32),
            pltpu.VMEM((rows, LANES), jnp.float32),
            pltpu.VMEM((rows, LANES), jnp.float32),
            pltpu.VMEM((2, rows, half), jnp.bfloat16),
            pltpu.VMEM((2, rows, half), jnp.bfloat16),
            pltpu.VMEM((2, GROUP * 8, half), jnp.bfloat16),
            pltpu.VMEM((2, GROUP * 8, half), jnp.bfloat16),
            pltpu.VMEM((DEVICES, 2, 8, rows), jnp.float32),
            pltpu.SemaphoreType.DMA((8,)),
            pltpu.SemaphoreType.DMA,
            pltpu.SemaphoreType.DMA,
            pltpu.SemaphoreType.DMA,
        ],
        compiler_params=pltpu.CompilerParams(
            collective_id=0, has_side_effects=True, vmem_limit_bytes=48 * 1024 * 1024
        ),
        name="spectra",
    )(voltages, halo, fir_taps, base, rot)
    return pl.pallas_call(
        gram_kernel,
        grid=(2, 4),
        out_shape=jax.ShapeDtypeStruct((8, 2, 512, 512), jnp.float32),
        in_specs=[pl.BlockSpec((DEVICES, 1, 8, rows), lambda p, q: (0, p, 0, 0))],
        out_specs=pl.BlockSpec((1, 2, 512, 512), lambda p, q: (2 * q + p, 0, 0, 0)),
        scratch_shapes=[
            pltpu.VMEM((8 * 512, LANES), jnp.float32),
            pltpu.VMEM((4, 4, 512, 2 * LANES), jnp.bfloat16),
        ],
        compiler_params=pltpu.CompilerParams(
            dimension_semantics=("arbitrary", "arbitrary"), vmem_limit_bytes=48 * 1024 * 1024
        ),
        name="gram",
    )(owned)


def solution(mesh):
    return jax.shard_map(
        body,
        mesh=mesh,
        in_specs=(P("chan", "tm"), P()),
        out_specs=P(("tm", "chan"), None, None, None),
        check_vma=False,
    )
```

```python
import functools

import jax
import jax.numpy as jnp
import numpy as np
from jax import lax
from jax.experimental import pallas as pl
from jax.experimental.pallas import tpu as pltpu
from jax.sharding import PartitionSpec as P

MESH = pl.DeviceIdType.MESH
DEVICES = 128
GROUP = 16
LANES = 128


def tables(frame, scale):
    half = frame // 2
    sample = np.arange(half)

    def angle(k):
        return 2.0 * np.pi * ((k[:, None] * sample) % frame) / frame

    base = []
    for parity in range(2):
        wave = angle(2 * np.arange(4) + parity)
        cos, sin = np.cos(wave) * scale, np.sin(wave) * scale
        base.append(np.stack([cos, -sin], axis=1).reshape(8, half))
        base.append(np.stack([-sin, -cos], axis=1).reshape(8, half))
    turn = angle(8 * np.arange(DEVICES))
    rot = np.stack([np.cos(turn), np.sin(turn)])
    return np.stack(base).astype(np.float32), rot.astype(np.float32)


def coordinates():
    tm = lax.axis_index("tm")
    chan = lax.axis_index("chan")
    return chan // 8, (chan // 2) % 4, (tm // 2) * 2 + chan % 2, tm % 2


def target(t, place):
    x, y, z, core = place
    x = (x + t) % 4
    y = (y + t // 4 + t) % 4
    z = (z + t // 16 + t // 4 + t) % 4
    core = (core + t // 64 + t) % 2
    return (z // 2) * 2 + core, (x * 4 + y) * 2 + z % 2


def split(value):
    high = value.astype(jnp.bfloat16)
    return high, (value - high.astype(jnp.float32)).astype(jnp.bfloat16)


def turned_dot(a, b):
    return lax.dot_general(a, b, (((1,), (1,)), ((), ())), preferred_element_type=jnp.float32)


def spectra_kernel(
    volt, taps_in, base_in, rot_in, out, taps, base, rot, vbuf, halo, even, odd, fh, fl, th, tl, buf,
    in_sem, send_sem, recv_sem, own_sem, halo_send, halo_recv,
):
    inputs = volt.shape[0]
    frame = taps_in.shape[1]
    half = frame // 2
    edge = halo.shape[1]
    tm_size = lax.axis_size("tm")
    my_tm = lax.axis_index("tm")
    spec = volt.shape[1] // frame
    place = coordinates()
    me = lax.axis_index("tm") * 32 + lax.axis_index("chan")

    pieces = 4
    width = volt.shape[1] // pieces
    loads = []
    for piece in range(pieces):
        loads.append(
            pltpu.make_async_copy(
                volt.at[:, pl.ds(piece * width, width)],
                vbuf.at[:, pl.ds(piece * width, width)],
                in_sem.at[piece],
            )
        )
    loads.append(pltpu.make_async_copy(taps_in, taps, in_sem.at[pieces]))
    later = [
        pltpu.make_async_copy(base_in, base, in_sem.at[pieces + 1]),
        pltpu.make_async_copy(rot_in, rot, in_sem.at[pieces + 2]),
    ]
    for load in loads + later:
        load.start()

    barrier = pltpu.get_barrier_semaphore()

    def greet(t, carry):
        other = (me + t) % DEVICES
        pl.semaphore_signal(barrier, 1, device_id=(other // 32, other % 32), device_id_type=MESH)
        return carry

    lax.fori_loop(1, DEVICES, greet, 0)
    for load in loads:
        load.wait()

    def filter_spectra(block, frames, first):
        low = pl.multiple_of(block * LANES, LANES)
        high = pl.multiple_of(half + block * LANES, LANES)
        weights = [
            (
                jnp.broadcast_to(taps[pl.ds(tap, 1), pl.ds(low, LANES)], (inputs, LANES)),
                jnp.broadcast_to(taps[pl.ds(tap, 1), pl.ds(high, LANES)], (inputs, LANES)),
            )
            for tap in range(4)
        ]
        past = []
        for step, (source, start) in enumerate(frames):
            now = (
                source[:, pl.ds(pl.multiple_of(start + low, LANES), LANES)],
                source[:, pl.ds(pl.multiple_of(start + high, LANES), LANES)],
            )
            past = [now] + past[:3]
            if step < 3:
                continue
            a = past[0][0] * weights[0][0]
            b = past[0][1] * weights[0][1]
            for tap in range(1, 4):
                a = a + past[tap][0] * weights[tap][0]
                b = b + past[tap][1] * weights[tap][1]
            even[block, pl.ds(first + step - 3, inputs, stride=spec), :] = a + b
            odd[block, pl.ds(first + step - 3, inputs, stride=spec), :] = a - b

    def main_block(block, carry):
        filter_spectra(block, [(vbuf, k * frame) for k in range(spec)], 3)
        return carry

    def edge_block(block, carry):
        filter_spectra(block, [(halo, k * frame) for k in range(3)] + [(vbuf, k * frame) for k in range(3)], 0)
        low = pl.multiple_of(block * LANES, LANES)
        for parity, source in enumerate((even, odd)):
            for start in range(0, inputs * spec, LANES):
                rows = pl.ds(start, LANES)
                upper, lower = split(source[block, rows, :])
                fh[parity, rows, pl.ds(low, LANES)] = upper
                fl[parity, rows, pl.ds(low, LANES)] = lower
        return carry

    blocks = half // LANES
    lax.fori_loop(0, blocks // 2, main_block, 0)
    for load in later:
        load.wait()
    pl.semaphore_wait(barrier, DEVICES - 1)
    pass_on = pltpu.make_async_remote_copy(
        src_ref=volt.at[:, pl.ds(volt.shape[1] - edge, edge)],
        dst_ref=halo,
        send_sem=halo_send,
        recv_sem=halo_recv,
        device_id=((my_tm + 1) % tm_size, lax.axis_index("chan")),
        device_id_type=MESH,
    )

    @pl.when(my_tm < tm_size - 1)
    def _():
        pass_on.start()

    @pl.when(my_tm == 0)
    def _():
        halo[...] = jnp.zeros_like(halo)

    lax.fori_loop(blocks // 2, blocks, main_block, 0)

    @pl.when(my_tm > 0)
    def _():
        pass_on.wait_recv()

    lax.fori_loop(0, blocks, edge_block, 0)

    @pl.when(my_tm < tm_size - 1)
    def _():
        pass_on.wait_send()

    def chunk(c, carry):
        def table_rows(pair, inner):
            rows = pl.ds(pl.multiple_of(pair * 16, 16), 16)
            turns = []
            for k in range(2):
                tm, chan = target(c * GROUP + pair * 2 + k, place)
                device = tm * 32 + chan
                turns.append((rot[0, pl.ds(device, 1), :], rot[1, pl.ds(device, 1), :]))
            for parity in range(2):
                value = jnp.concatenate(
                    [base[2 * parity] * cos + base[2 * parity + 1] * sin for cos, sin in turns], axis=0
                )
                high, low = split(value)
                th[parity, rows, :] = high
                tl[parity, rows, :] = low
            return inner

        lax.fori_loop(0, GROUP // 2, table_rows, 0)
        slots = pl.ds(c * GROUP, GROUP)
        for parity in range(2):
            high = fh[parity]
            value = turned_dot(th[parity], high) + turned_dot(tl[parity], high) + turned_dot(th[parity], fl[parity])
            buf[slots, parity] = value.reshape(GROUP, 8, inputs * spec)

        def send(k, inner):
            t = c * GROUP + k

            @pl.when(t > 0)
            def _():
                pltpu.make_async_remote_copy(
                    src_ref=buf.at[t],
                    dst_ref=out.at[me],
                    send_sem=send_sem,
                    recv_sem=recv_sem,
                    device_id=target(t, place),
                    device_id_type=MESH,
                ).start()

            return inner

        lax.fori_loop(0, GROUP, send, 0)
        return carry

    lax.fori_loop(0, DEVICES // GROUP, chunk, 0)
    own = pltpu.make_async_copy(buf.at[0], out.at[me], own_sem)
    own.start()
    own.wait()
    rest = pl.ds(0, DEVICES - 1)
    pltpu.make_async_remote_copy(
        src_ref=buf.at[rest],
        dst_ref=out.at[rest],
        send_sem=send_sem,
        recv_sem=recv_sem,
        device_id=target(1, place),
        device_id_type=MESH,
    ).wait()


def regroup(blocks, lane):
    quarter = lane // 32

    def pick(choices):
        low = jnp.where(quarter == 0, choices[0], choices[1])
        high = jnp.where(quarter == 2, choices[2], choices[3])
        return jnp.where(quarter < 2, low, high)

    shifted = []
    for shift in range(4):
        mixed = pick([blocks[(a + shift) % 4] for a in range(4)])
        shifted.append(pltpu.roll(mixed, 32 * shift, 1) if shift else mixed)
    return [pick([shifted[(tm - a) % 4] for tm in range(4)]) for a in range(4)]


def gram_kernel(owned, out, held, pairs):
    @pl.when(pl.program_id(1) == 0)
    def _():
        lane = lax.broadcasted_iota(jnp.int32, (8, LANES), 1)

        def sender(n, carry):
            for g in range(4):
                lanes = pl.ds(g * LANES, LANES)
                parts = regroup([owned[tm * 32 + n, 0, :, lanes] for tm in range(4)], lane)
                for a in range(4):
                    held[pl.ds(pl.multiple_of((n * 16 + g * 4 + a) * 8, 8), 8), :] = parts[a]
            return carry

        lax.fori_loop(0, 32, sender, 0, unroll=2)

        def channel(q, carry):
            re_h, re_l = split(held[pl.ds(q * 2, 512, stride=8), :])
            im_h, im_l = split(held[pl.ds(q * 2 + 1, 512, stride=8), :])
            for kind, (left, right) in enumerate(((re_h, im_h), (re_l, im_l), (im_h, -re_h), (im_l, -re_l))):
                pairs[q, kind, :, :LANES] = left
                pairs[q, kind, :, LANES:] = right
            return carry

        lax.fori_loop(0, 4, channel, 0)

    q = pl.program_id(1)
    right_h, right_l, turned_h, turned_l = (pairs[q, kind] for kind in range(4))
    left = jnp.concatenate([right_h, turned_h, right_l, turned_l], axis=0)
    wide = turned_dot(left, right_h)
    fine = turned_dot(left[:1024], right_l)
    for part in range(2):
        here = slice(part * 512, (part + 1) * 512)
        there = slice((part + 2) * 512, (part + 3) * 512)
        out[0, part] = wide[here] + wide[there] + fine[here]


def body(voltages, fir_taps):
    inputs = voltages.shape[0]
    frame = fir_taps.shape[1]
    half = frame // 2
    edge = (fir_taps.shape[0] - 1) * frame
    spec = voltages.shape[1] // frame
    rows = inputs * spec
    base, rot = tables(frame, 1.0 / 512.0)
    anywhere = pl.BlockSpec(memory_space=pl.ANY)
    owned = pl.pallas_call(
        spectra_kernel,
        out_shape=jax.ShapeDtypeStruct((DEVICES, 2, 8, rows), jnp.float32),
        in_specs=[pl.BlockSpec(memory_space=pltpu.HBM)] * 4,
        out_specs=anywhere,
        scratch_shapes=[
            pltpu.VMEM(fir_taps.shape, jnp.float32),
            pltpu.VMEM(base.shape, jnp.float32),
            pltpu.VMEM(rot.shape, jnp.float32),
            pltpu.VMEM(voltages.shape, jnp.float32),
            pltpu.VMEM((inputs, edge), jnp.float32),
            pltpu.VMEM((half // LANES, rows, LANES), jnp.float32),
            pltpu.VMEM((half // LANES, rows, LANES), jnp.float32),
            pltpu.VMEM((2, rows, half), jnp.bfloat16),
            pltpu.VMEM((2, rows, half), jnp.bfloat16),
            pltpu.VMEM((2, GROUP * 8, half), jnp.bfloat16),
            pltpu.VMEM((2, GROUP * 8, half), jnp.bfloat16),
            pltpu.VMEM((DEVICES, 2, 8, rows), jnp.float32),
            pltpu.SemaphoreType.DMA((7,)),
            pltpu.SemaphoreType.DMA,
            pltpu.SemaphoreType.DMA,
            pltpu.SemaphoreType.DMA,
            pltpu.SemaphoreType.DMA,
            pltpu.SemaphoreType.DMA,
        ],
        compiler_params=pltpu.CompilerParams(
            collective_id=0, has_side_effects=True, vmem_limit_bytes=60 * 1024 * 1024
        ),
        name="spectra",
    )(voltages, fir_taps, base, rot)
    return pl.pallas_call(
        gram_kernel,
        grid=(2, 4),
        out_shape=jax.ShapeDtypeStruct((8, 2, 512, 512), jnp.float32),
        in_specs=[pl.BlockSpec((DEVICES, 1, 8, rows), lambda p, q: (0, p, 0, 0))],
        out_specs=pl.BlockSpec((1, 2, 512, 512), lambda p, q: (2 * q + p, 0, 0, 0)),
        scratch_shapes=[
            pltpu.VMEM((8 * 512, LANES), jnp.float32),
            pltpu.VMEM((4, 4, 512, 2 * LANES), jnp.bfloat16),
        ],
        compiler_params=pltpu.CompilerParams(
            dimension_semantics=("arbitrary", "arbitrary"), vmem_limit_bytes=60 * 1024 * 1024
        ),
        name="gram",
    )(owned)


def solution(mesh):
    return jax.shard_map(
        body,
        mesh=mesh,
        in_specs=(P("chan", "tm"), P()),
        out_specs=P(("tm", "chan"), None, None, None),
        check_vma=False,
    )
```

```python
import functools

import jax
import jax.numpy as jnp
import numpy as np
from jax import lax
from jax.experimental import pallas as pl
from jax.experimental.pallas import tpu as pltpu
from jax.sharding import PartitionSpec as P

MESH = pl.DeviceIdType.MESH
DEVICES = 128
GROUP = 16
LANES = 128


def tables(frame, scale):
    half = frame // 2
    sample = np.arange(half)

    def angle(k):
        return 2.0 * np.pi * ((k[:, None] * sample) % frame) / frame

    base = []
    for parity in range(2):
        wave = angle(2 * np.arange(4) + parity)
        cos, sin = np.cos(wave) * scale, np.sin(wave) * scale
        base.append(np.stack([cos, -sin], axis=1).reshape(8, half))
        base.append(np.stack([-sin, -cos], axis=1).reshape(8, half))
    turn = angle(8 * np.arange(DEVICES))
    rot = np.stack([np.cos(turn), np.sin(turn)])
    return np.stack(base).astype(np.float32), rot.astype(np.float32)


def coordinates():
    tm = lax.axis_index("tm")
    chan = lax.axis_index("chan")
    return chan // 8, (chan // 2) % 4, (tm // 2) * 2 + chan % 2, tm % 2


def target(t, place):
    x, y, z, core = place
    x = (x + t) % 4
    y = (y + t // 4 + t) % 4
    z = (z + t // 16 + t // 4 + t) % 4
    core = (core + t // 64 + t) % 2
    return (z // 2) * 2 + core, (x * 4 + y) * 2 + z % 2


def split(value):
    high = value.astype(jnp.bfloat16)
    return high, (value - high.astype(jnp.float32)).astype(jnp.bfloat16)


def turned_dot(a, b):
    return lax.dot_general(a, b, (((1,), (1,)), ((), ())), preferred_element_type=jnp.float32)


def spectra_kernel(
    volt, taps_in, base_in, rot_in, out, taps, base, rot, vbuf, halo, even, odd, fh, fl, th, tl, buf,
    in_sem, send_sem, recv_sem, own_sem, halo_send, halo_recv,
):
    inputs = volt.shape[0]
    frame = taps_in.shape[1]
    half = frame // 2
    edge = halo.shape[1]
    tm_size = lax.axis_size("tm")
    my_tm = lax.axis_index("tm")
    spec = volt.shape[1] // frame
    place = coordinates()
    me = lax.axis_index("tm") * 32 + lax.axis_index("chan")

    pieces = 4
    width = volt.shape[1] // pieces
    loads = []
    for piece in range(pieces):
        loads.append(
            pltpu.make_async_copy(
                volt.at[:, pl.ds(piece * width, width)],
                vbuf.at[:, pl.ds(piece * width, width)],
                in_sem.at[piece],
            )
        )
    loads.append(pltpu.make_async_copy(taps_in, taps, in_sem.at[pieces]))
    later = [
        pltpu.make_async_copy(base_in, base, in_sem.at[pieces + 1]),
        pltpu.make_async_copy(rot_in, rot, in_sem.at[pieces + 2]),
    ]
    for load in loads + later:
        load.start()

    barrier = pltpu.get_barrier_semaphore()

    def greet(t, carry):
        other = (me + t) % DEVICES
        pl.semaphore_signal(barrier, 1, device_id=(other // 32, other % 32), device_id_type=MESH)
        return carry

    lax.fori_loop(1, DEVICES, greet, 0)
    for load in loads:
        load.wait()

    def filter_spectra(block, frames, first):
        low = pl.multiple_of(block * LANES, LANES)
        high = pl.multiple_of(half + block * LANES, LANES)
        weights = [
            (
                jnp.broadcast_to(taps[pl.ds(tap, 1), pl.ds(low, LANES)], (inputs, LANES)),
                jnp.broadcast_to(taps[pl.ds(tap, 1), pl.ds(high, LANES)], (inputs, LANES)),
            )
            for tap in range(4)
        ]
        past = []
        for step, (source, start) in enumerate(frames):
            now = (
                source[:, pl.ds(pl.multiple_of(start + low, LANES), LANES)],
                source[:, pl.ds(pl.multiple_of(start + high, LANES), LANES)],
            )
            past = [now] + past[:3]
            if step < 3:
                continue
            a = past[0][0] * weights[0][0]
            b = past[0][1] * weights[0][1]
            for tap in range(1, 4):
                a = a + past[tap][0] * weights[tap][0]
                b = b + past[tap][1] * weights[tap][1]
            even[block, pl.ds(first + step - 3, inputs, stride=spec), :] = a + b
            odd[block, pl.ds(first + step - 3, inputs, stride=spec), :] = a - b

    def main_block(block, carry):
        filter_spectra(block, [(vbuf, k * frame) for k in range(spec)], 3)
        return carry

    def edge_block(block, carry):
        filter_spectra(block, [(halo, k * frame) for k in range(3)] + [(vbuf, k * frame) for k in range(3)], 0)
        low = pl.multiple_of(block * LANES, LANES)
        for parity, source in enumerate((even, odd)):
            for start in range(0, inputs * spec, LANES):
                rows = pl.ds(start, LANES)
                upper, lower = split(source[block, rows, :])
                fh[parity, rows, pl.ds(low, LANES)] = upper
                fl[parity, rows, pl.ds(low, LANES)] = lower
        return carry

    blocks = half // LANES
    lax.fori_loop(0, blocks // 2, main_block, 0)
    for load in later:
        load.wait()
    pl.semaphore_wait(barrier, DEVICES - 1)
    pass_on = pltpu.make_async_remote_copy(
        src_ref=volt.at[:, pl.ds(volt.shape[1] - edge, edge)],
        dst_ref=halo,
        send_sem=halo_send,
        recv_sem=halo_recv,
        device_id=((my_tm + 1) % tm_size, lax.axis_index("chan")),
        device_id_type=MESH,
    )

    @pl.when(my_tm < tm_size - 1)
    def _():
        pass_on.start()

    @pl.when(my_tm == 0)
    def _():
        halo[...] = jnp.zeros_like(halo)

    lax.fori_loop(blocks // 2, blocks, main_block, 0)

    @pl.when(my_tm > 0)
    def _():
        pass_on.wait_recv()

    lax.fori_loop(0, blocks, edge_block, 0)

    @pl.when(my_tm < tm_size - 1)
    def _():
        pass_on.wait_send()

    def chunk(c, carry):
        def table_rows(pair, inner):
            rows = pl.ds(pl.multiple_of(pair * 16, 16), 16)
            turns = []
            for k in range(2):
                tm, chan = target(c * GROUP + pair * 2 + k, place)
                device = tm * 32 + chan
                turns.append((rot[0, pl.ds(device, 1), :], rot[1, pl.ds(device, 1), :]))
            for parity in range(2):
                value = jnp.concatenate(
                    [base[2 * parity] * cos + base[2 * parity + 1] * sin for cos, sin in turns], axis=0
                )
                high, low = split(value)
                th[parity, rows, :] = high
                tl[parity, rows, :] = low
            return inner

        lax.fori_loop(0, GROUP // 2, table_rows, 0)
        slots = pl.ds(c * GROUP, GROUP)
        for parity in range(2):
            high = fh[parity]
            value = turned_dot(th[parity], high) + turned_dot(tl[parity], high) + turned_dot(th[parity], fl[parity])
            buf[slots, parity] = value.reshape(GROUP, 8, inputs * spec)

        def send(k, inner):
            t = c * GROUP + k

            @pl.when(t > 0)
            def _():
                pltpu.make_async_remote_copy(
                    src_ref=buf.at[t],
                    dst_ref=out.at[me],
                    send_sem=send_sem,
                    recv_sem=recv_sem,
                    device_id=target(t, place),
                    device_id_type=MESH,
                ).start()

            return inner

        lax.fori_loop(0, GROUP, send, 0)
        return carry

    lax.fori_loop(0, DEVICES // GROUP, chunk, 0)
    own = pltpu.make_async_copy(buf.at[0], out.at[me], own_sem)
    own.start()
    own.wait()
    rest = pl.ds(0, DEVICES - 1)
    pltpu.make_async_remote_copy(
        src_ref=buf.at[rest],
        dst_ref=out.at[rest],
        send_sem=send_sem,
        recv_sem=recv_sem,
        device_id=target(1, place),
        device_id_type=MESH,
    ).wait()


def regroup(blocks, lane):
    quarter = lane // 32

    def pick(choices):
        low = jnp.where(quarter == 0, choices[0], choices[1])
        high = jnp.where(quarter == 2, choices[2], choices[3])
        return jnp.where(quarter < 2, low, high)

    shifted = []
    for shift in range(4):
        mixed = pick([blocks[(a + shift) % 4] for a in range(4)])
        shifted.append(pltpu.roll(mixed, 32 * shift, 1) if shift else mixed)
    return [pick([shifted[(tm - a) % 4] for tm in range(4)]) for a in range(4)]


def gram_kernel(source, out, held, pairs, owned, sem):
    p = pl.program_id(0)

    def fetch(p, piece):
        rows = pl.ds(piece * 8, 8)
        return pltpu.make_async_copy(source.at[:, rows, p], owned.at[p, :, rows], sem.at[p, piece])

    @pl.when((p == 0) & (pl.program_id(1) == 0))
    def _():
        for part in range(2):
            for piece in range(4):
                fetch(part, piece).start()

    @pl.when(pl.program_id(1) == 0)
    def _():
        lane = lax.broadcasted_iota(jnp.int32, (8, LANES), 1)

        def sender(n, carry):
            for g in range(4):
                lanes = pl.ds(g * LANES, LANES)
                parts = regroup([owned[p, tm, n, :, lanes] for tm in range(4)], lane)
                for a in range(4):
                    held[pl.ds(pl.multiple_of((n * 16 + g * 4 + a) * 8, 8), 8), :] = parts[a]
            return carry

        for piece in range(4):
            fetch(p, piece).wait()
            lax.fori_loop(piece * 8, piece * 8 + 8, sender, 0, unroll=2)

        def channel(q, carry):
            re_h, re_l = split(held[pl.ds(q * 2, 512, stride=8), :])
            im_h, im_l = split(held[pl.ds(q * 2 + 1, 512, stride=8), :])
            for kind, (left, right) in enumerate(((re_h, im_h), (re_l, im_l), (im_h, -re_h), (im_l, -re_l))):
                pairs[q, kind, :, :LANES] = left
                pairs[q, kind, :, LANES:] = right
            return carry

        lax.fori_loop(0, 4, channel, 0)

    q = pl.program_id(1)
    right_h, right_l, turned_h, turned_l = (pairs[q, kind] for kind in range(4))
    left = jnp.concatenate([right_h, turned_h, right_l, turned_l], axis=0)
    wide = turned_dot(left, right_h)
    fine = turned_dot(left[:1024], right_l)
    for part in range(2):
        here = slice(part * 512, (part + 1) * 512)
        there = slice((part + 2) * 512, (part + 3) * 512)
        out[0, part] = wide[here] + wide[there] + fine[here]


def body(voltages, fir_taps):
    inputs = voltages.shape[0]
    frame = fir_taps.shape[1]
    half = frame // 2
    edge = (fir_taps.shape[0] - 1) * frame
    spec = voltages.shape[1] // frame
    rows = inputs * spec
    base, rot = tables(frame, 1.0 / 512.0)
    anywhere = pl.BlockSpec(memory_space=pl.ANY)
    owned = pl.pallas_call(
        spectra_kernel,
        out_shape=jax.ShapeDtypeStruct((DEVICES, 2, 8, rows), jnp.float32),
        in_specs=[pl.BlockSpec(memory_space=pltpu.HBM)] * 4,
        out_specs=anywhere,
        scratch_shapes=[
            pltpu.VMEM(fir_taps.shape, jnp.float32),
            pltpu.VMEM(base.shape, jnp.float32),
            pltpu.VMEM(rot.shape, jnp.float32),
            pltpu.VMEM(voltages.shape, jnp.float32),
            pltpu.VMEM((inputs, edge), jnp.float32),
            pltpu.VMEM((half // LANES, rows, LANES), jnp.float32),
            pltpu.VMEM((half // LANES, rows, LANES), jnp.float32),
            pltpu.VMEM((2, rows, half), jnp.bfloat16),
            pltpu.VMEM((2, rows, half), jnp.bfloat16),
            pltpu.VMEM((2, GROUP * 8, half), jnp.bfloat16),
            pltpu.VMEM((2, GROUP * 8, half), jnp.bfloat16),
            pltpu.VMEM((DEVICES, 2, 8, rows), jnp.float32),
            pltpu.SemaphoreType.DMA((7,)),
            pltpu.SemaphoreType.DMA,
            pltpu.SemaphoreType.DMA,
            pltpu.SemaphoreType.DMA,
            pltpu.SemaphoreType.DMA,
            pltpu.SemaphoreType.DMA,
        ],
        compiler_params=pltpu.CompilerParams(
            collective_id=0, has_side_effects=True, vmem_limit_bytes=60 * 1024 * 1024
        ),
        name="spectra",
    )(voltages, fir_taps, base, rot)
    return pl.pallas_call(
        gram_kernel,
        grid=(2, 4),
        out_shape=jax.ShapeDtypeStruct((8, 2, 512, 512), jnp.float32),
        in_specs=[pl.BlockSpec(memory_space=pltpu.HBM)],
        out_specs=pl.BlockSpec((1, 2, 512, 512), lambda p, q: (2 * q + p, 0, 0, 0)),
        scratch_shapes=[
            pltpu.VMEM((8 * 512, LANES), jnp.float32),
            pltpu.VMEM((4, 4, 512, 2 * LANES), jnp.bfloat16),
            pltpu.VMEM((2, 4, 32, 8, rows), jnp.float32),
            pltpu.SemaphoreType.DMA((2, 4)),
        ],
        compiler_params=pltpu.CompilerParams(
            dimension_semantics=("arbitrary", "arbitrary"), vmem_limit_bytes=60 * 1024 * 1024
        ),
        name="gram",
    )(owned.reshape(4, 32, 2, 8, rows))


def solution(mesh):
    return jax.shard_map(
        body,
        mesh=mesh,
        in_specs=(P("chan", "tm"), P()),
        out_specs=P(("tm", "chan"), None, None, None),
        check_vma=False,
    )
```
